32 devices in a mesh: groups: 2 (over y), dp: 16 (over z, x, core).
Axes of the slice: x: 2, y: 2, z: 4, core: 2. Of those that a mesh axis runs over, the one named last changes fastest.
Arguments:
- state: bfloat16 [32, 128, 64, 128], P(('groups', 'dp')), parts along dimension 0, may hold values from -6 to 6
- x_in: bfloat16 [32, 8192], P(('groups', 'dp')), parts along dimension 0, may hold values from -6 to 6
- z_gate: bfloat16 [32, 8192], P(('groups', 'dp')), parts along dimension 0, may hold values from -6 to 6
- b_in: bfloat16 [32, 512], P(('groups', 'dp')), parts along dimension 0, may hold values from -6 to 6
- c_in: bfloat16 [32, 512], P(('groups', 'dp')), parts along dimension 0, may hold values from -0.59765625 to 0.59765625
- dt_raw: float32 [32, 128], P(('groups', 'dp')), parts along dimension 0, may hold values from -5 to 5
- dt_bias: float32 [128], replicated, may hold values from -3 to 0.5
- a_log: float32 [128], replicated, may hold values from -1 to 1.5
- d_skip: float32 [128], replicated, may hold values from 0.3 to 1.7
- norm_gain: float32 [8192], replicated, may hold values from 0.1 to 1.9
- out_proj: bfloat16 [8192, 8192], P('dp'), may hold values from -0.0625 to 0.0625
- active: int32 [32], P(('groups', 'dp')), parts along dimension 0, may hold values from 0 to 1
- plan: int32 [16, 2], P('groups'), parts along dimension 0, may hold values from 0 to 15, as said below
Outputs:
- mixed: bfloat16 [32, 8192], P(('groups', 'dp')), parts along dimension 0
- new_state: bfloat16 [32, 128, 64, 128], P(('groups', 'dp')), parts along dimension 0
The draws below stay inside these ranges and needn't reach their ends.
There are 2 independent parts, one for each index of `groups`. The reference program is written for one: setup_inputs(seed, part) draws one part's arguments, and reference() takes and returns one part's arrays. A program takes and returns all parts, laid end to end along the dimension named above; an argument that names none is the same for every part. Nothing has to cross between parts.
Inputs may be any that keep to these rules, and one draw needn't show every extreme that they name: `plan`: exactly 8 moves. Source slots are distinct and live in active; destination slots are distinct and not live in active. Slot k belongs to device k. Each device holds the source of at most one move and the destination of at most one, never both; both bounds are reached.
All inputs are finite; a program needn't handle non-finite values.
Results may differ from the reference program's by a relative error of at most 0.0049.
Values may be sent and summed in bfloat16 or wider, within the bound.
No kernel may reach another device: no remote copies, remote signals or barrier semaphores. Data moves between devices by JAX's collectives and lax.ppermute only.
A program may use at most 64 MiB of HBM per device.

```python
import jax
import jax.numpy as jnp
from jax import lax

D = 8192
H = 128
P_SIZE = 64
N = 128
G = 4
SLOTS = 1
SLOTS_ALL = 16
MOVES = 8


def plan_tables(key):
    base = jax.random.fold_in(key, 4711)
    devices = SLOTS_ALL // SLOTS
    order = jax.random.permutation(jax.random.fold_in(base, 1), devices).astype(jnp.int32)
    crowded = order[:MOVES]
    holes = order[MOVES:2 * MOVES]
    src_slot = jax.random.randint(jax.random.fold_in(base, 2), (MOVES,), 0, SLOTS).astype(jnp.int32)
    dst_slot = jax.random.randint(jax.random.fold_in(base, 3), (MOVES,), 0, SLOTS).astype(jnp.int32)
    source = crowded * SLOTS + src_slot
    target = holes * SLOTS + dst_slot
    bits = jax.random.randint(jax.random.fold_in(base, 4), (SLOTS_ALL,), 0, 2).astype(jnp.int32)
    is_crowded = jnp.zeros((devices,), jnp.int32).at[crowded].set(1)
    slot_owner = jnp.arange(SLOTS_ALL, dtype=jnp.int32) // SLOTS
    active = jnp.where(is_crowded[slot_owner] > 0, 1, bits).astype(jnp.int32)
    active = active.at[target].set(0)
    plan = jnp.stack([source, target], axis=1).astype(jnp.int32)
    return (active, plan)


def draw_active(key, part):
    return plan_tables(key)[0]


def draw_plan(key, part):
    return plan_tables(key)[1]


def level_of(stream_key, shape, split, least, top_value):
    loudness, own = 1.0, jax.random.fold_in(stream_key, 6)
    for position, parts in split:
        heights = jnp.exp(jax.random.uniform(jax.random.fold_in(own, position), (parts,), jnp.float32, least / len(split), top_value / len(split)))
        loudness = loudness * jnp.repeat(heights, shape[position] // parts).reshape([-1 if axis == position else 1 for axis in range(len(shape))])
    return loudness


def centred(rng, shape, scale, limit, cuts=(), kind=jnp.bfloat16):
    drawn = jax.random.normal(rng, shape, jnp.float32) * scale
    if len(cuts) > 0:
        drawn = level_of(rng, shape, cuts, -0.22, 0.18) * drawn
    return jnp.clip(drawn, min=-limit, max=limit).astype(kind)


def setup_inputs(seed: int = 0, part: int = 0) -> dict:
    keys = jax.random.split(jax.random.key(seed), 14)
    part_splits = jax.random.split(jax.random.fold_in(keys[13], part), 14)
    return {
        "state": centred(part_splits[0], (SLOTS_ALL, H, P_SIZE, N), 1.0, 6.0, ((0, 16),)),
        "x_in": centred(part_splits[1], (SLOTS_ALL, H * P_SIZE), 1.0, 6.0, ((0, 16),)),
        "z_gate": centred(part_splits[2], (SLOTS_ALL, H * P_SIZE), 1.5, 6.0, ((0, 16),)),
        "b_in": centred(part_splits[3], (SLOTS_ALL, G * N), 1.0, 6.0, ((0, 16),)),
        "c_in": centred(part_splits[4], (SLOTS_ALL, G * N), 0.09, 0.59765625, ((0, 16),)),
        "dt_raw": centred(part_splits[5], (SLOTS_ALL, H), 1.0, 5.0, ((0, 16),), jnp.float32),
        "dt_bias": jnp.clip(jax.random.uniform(keys[6], (H,), jnp.float32, -3.0, 0.5), -3.0, 0.5),
        "a_log": jnp.clip(jax.random.uniform(keys[7], (H,), jnp.float32, -1.0, 1.5), -1.0, 1.5),
        "d_skip": jnp.clip(jax.random.uniform(keys[8], (H,), jnp.float32, 0.3, 1.7), 0.3, 1.7),
        "norm_gain": jnp.clip(1.0 + 0.18 * jax.random.normal(keys[9], (H * P_SIZE,), jnp.float32), 0.1, 1.9),
        "out_proj": centred(keys[10], (H * P_SIZE, D), (H * P_SIZE) ** -0.5, 0.0625, ((0, 16),)),
        "active": draw_active(jax.random.fold_in(jax.random.fold_in(keys[13], part), 71), part),
        "plan": draw_plan(jax.random.fold_in(jax.random.fold_in(keys[13], part), 71), part),
    }


def update_row(st, xr, zr, br, cr, dtr, dt_bias, a_log, d_skip, norm_gain):
    step_size = jax.nn.softplus(dtr + dt_bias)
    decay = jnp.exp(-jnp.exp(a_log) * step_size)
    inputs = xr.astype(jnp.float32).reshape(H, P_SIZE)
    b_heads = jnp.repeat(br.astype(jnp.float32).reshape(G, N), H // G, axis=0)
    c_heads = jnp.repeat(cr.astype(jnp.float32).reshape(G, N), H // G, axis=0)
    fresh = decay[:, None, None] * st.astype(jnp.float32) + (step_size[:, None] * inputs)[:, :, None] * b_heads[:, None, :]
    y_out = lax.optimization_barrier(jnp.sum(fresh * c_heads[:, None, :], axis=2)) + d_skip[:, None] * inputs
    gated = (y_out.reshape(-1) * jax.nn.silu(zr.astype(jnp.float32))).reshape(G, -1)
    factor = lax.rsqrt(lax.optimization_barrier(jnp.mean(gated * gated, axis=1, keepdims=True)) + 1e-05)
    normed = ((gated * factor).reshape(-1) * norm_gain).astype(jnp.bfloat16)
    return (fresh.astype(jnp.bfloat16), normed)

def reference(state, x_in, z_gate, b_in, c_in, dt_raw, dt_bias, a_log, d_skip, norm_gain, out_proj, active, plan):
    source = plan[:, 0]
    target = plan[:, 1]
    moved = jnp.take(state, source, axis=0)
    placed = state.at[target].set(moved)
    live = active.at[source].set(0).at[target].set(1)

    def one_row(items):
        return update_row(items[0], items[1], items[2], items[3], items[4], items[5], dt_bias, a_log, d_skip, norm_gain)
    fresh, normed = lax.map(one_row, (placed, x_in, z_gate, b_in, c_in, dt_raw))
    mixed = jnp.dot(normed, out_proj, preferred_element_type=jnp.float32).astype(jnp.bfloat16)
    mixed = jnp.where(live[:, None] > 0, mixed, jnp.zeros((), jnp.bfloat16))
    new_state = jnp.where(live[:, None, None, None] > 0, fresh, jnp.zeros((), jnp.bfloat16))
    return (mixed, new_state)
```

```python
import functools

import jax
import jax.numpy as jnp
from jax import lax
from jax.experimental import pallas as pl
from jax.experimental.pallas import tpu as pltpu
from jax.sharding import PartitionSpec as P

AXIS = "dp"
LANES = 128
MOST_PATTERNS = 32
F32 = jnp.float32
BF16 = jnp.bfloat16


def pair_switch(index, devices, array):
    def branch(distance, low_sends):
        pairs = [(i, i ^ distance) for i in range(devices) if (i < (i ^ distance)) == low_sends]
        return lambda a: lax.ppermute(a, AXIS, pairs)

    branches = [branch(d, low) for d in range(1, devices) for low in (True, False)]
    return lax.switch(index, branches, array)


def spread_and_collect(state, source, target, devices):
    ids = jnp.arange(devices, dtype=jnp.int32)
    matches = target[:, None] == ids[None, :]
    sender_of = jnp.sum(jnp.where(matches, source[:, None], 0), axis=0)
    has_sender = jnp.any(matches, axis=0)
    view = lax.all_to_all(state, AXIS, split_axis=1, concat_axis=0, tiled=True)
    routed = jnp.where(
        has_sender[:, None, None, None], jnp.take(view, sender_of, axis=0), jnp.zeros((), state.dtype)
    )
    return lax.all_to_all(routed, AXIS, split_axis=0, concat_axis=1, tiled=True)


def mix_kernel(live, s, x, z, b, c, per_head, gain, out):
    heads, p_size, n = s.shape
    width = heads * p_size
    c16 = jnp.broadcast_to(c[...], (16, n))
    t = lax.dot_general(
        c16, s[...].reshape(width, n), (((1,), (1,)), ((), ())), preferred_element_type=F32
    )[0:1]
    bc = jnp.sum(b[...].astype(F32) * c[...].astype(F32), axis=1, keepdims=True)
    xf = x[...].astype(F32)
    y = per_head[0:1] * t + (per_head[1:2] * xf) * bc + per_head[2:3] * xf
    gated = y * jax.nn.silu(z[...].astype(F32))
    factor = lax.rsqrt(jnp.mean(gated * gated, axis=1, keepdims=True) + 1e-05)
    normed = jnp.where(live[0] > 0, gated * factor * gain[...], 0.0)
    for q in range(width // LANES):
        out[q : q + 1, :] = normed[:, q * LANES : (q + 1) * LANES].astype(BF16)


def update_kernel(live, decay, s, x, b, per_head, out):
    heads, p_size, n = s.shape
    g = pl.program_id(0)
    dx = per_head[1:2] * x[...].astype(F32)
    first = dx.astype(BF16)
    rest = dx - first.astype(F32)
    second = rest.astype(BF16)
    third = (rest - second.astype(F32)).astype(BF16)
    row = lax.broadcasted_iota(jnp.int32, (16, dx.shape[1]), 0)
    terms = jnp.where(
        row == 0,
        first.astype(F32),
        jnp.where(row == 1, second.astype(F32), jnp.where(row == 2, third.astype(F32), 0.0)),
    ).astype(BF16)
    outer = lax.dot_general(
        terms, jnp.broadcast_to(b[...], (16, n)), (((0,), (0,)), ((), ())), preferred_element_type=F32
    )
    for h in range(heads):
        fresh = decay[g * heads + h] * s[h].astype(F32) + outer[h * p_size : (h + 1) * p_size]
        out[h] = jnp.where(live[0] > 0, fresh, 0.0).astype(BF16)


def project_kernel(rows, w, out):
    depth, lanes = rows.shape[1:]
    total = None
    for r in range(depth):
        part = jnp.dot(rows[:, r, :], w[r * lanes : (r + 1) * lanes, :], preferred_element_type=F32)
        total = part if total is None else total + part
    for j in range(w.shape[1] // LANES):
        out[:, j, :] = total[:, j * LANES : (j + 1) * LANES].astype(out.dtype)


def sum_kernel(parts, out):
    total = jnp.sum(parts[...].astype(F32), axis=0).astype(BF16)
    for q in range(total.shape[0]):
        out[0:1, q * LANES : (q + 1) * LANES] = total[q : q + 1, :]


def local(
    state,
    x_in,
    z_gate,
    b_in,
    c_in,
    dt_raw,
    dt_bias,
    a_log,
    d_skip,
    norm_gain,
    out_proj,
    active,
    plan,
):
    devices = lax.axis_size(AXIS)
    me = lax.axis_index(AXIS)
    heads, p_size, n = state.shape[1:]
    groups = b_in.shape[1] // n
    width = heads * p_size
    columns = out_proj.shape[1]
    source, target = plan[:, 0], plan[:, 1]
    partner = jnp.sum(jnp.where(source == me, target, 0) + jnp.where(target == me, source, 0))
    sends = jnp.any(source == me)
    live = jnp.where(sends, 0, 1).astype(jnp.int32).reshape(1)

    if 2 * (devices - 1) <= MOST_PATTERNS and devices & (devices - 1) == 0:
        low_sends = sends == (me < partner)
        index = 2 * ((me ^ partner) - 1) + jnp.where(low_sends, 0, 1)
        came = pair_switch(index, devices, state)
    else:
        came = spread_and_collect(state, source, target, devices)
    came = came.reshape(heads, p_size, n)

    step = jax.nn.softplus(dt_raw[0] + dt_bias)
    decay = jnp.exp(-jnp.exp(a_log) * step)
    per_head = jnp.repeat(jnp.stack([decay, step, d_skip]), p_size, axis=1)
    gain = norm_gain.reshape(1, width)

    smem = pl.BlockSpec(memory_space=pltpu.SMEM)
    of_group = width // groups
    state_spec = pl.BlockSpec((heads // groups, p_size, n), lambda g: (g, 0, 0))
    row_spec = pl.BlockSpec((1, of_group), lambda g: (0, g))
    n_spec = pl.BlockSpec((1, n), lambda g: (0, g))
    head_spec = pl.BlockSpec((3, of_group), lambda g: (0, g))

    normed = pl.pallas_call(
        mix_kernel,
        name="mix",
        grid=(groups,),
        in_specs=[smem, state_spec, row_spec, row_spec, n_spec, n_spec, head_spec, row_spec],
        out_specs=pl.BlockSpec((of_group // LANES, LANES), lambda g: (g, 0)),
        out_shape=jax.ShapeDtypeStruct((width // LANES, LANES), BF16),
    )(live, came, x_in, z_gate, b_in, c_in, per_head, gain)

    block = width // devices
    lanes = min(block, LANES)
    mine = lax.all_to_all(
        normed.reshape(devices, block // lanes, lanes), AXIS, split_axis=0, concat_axis=0, tiled=True
    )

    new_state = pl.pallas_call(
        update_kernel,
        name="update",
        grid=(groups,),
        in_specs=[smem, smem, state_spec, row_spec, n_spec, head_spec],
        out_specs=state_spec,
        out_shape=jax.ShapeDtypeStruct((heads, p_size, n), BF16),
    )(live, decay, came, x_in, b_in, per_head)

    tile = 1024
    partial = pl.pallas_call(
        project_kernel,
        name="project",
        grid=(columns // tile,),
        in_specs=[
            pl.BlockSpec((devices, block // lanes, lanes), lambda i: (0, 0, 0)),
            pl.BlockSpec((block, tile), lambda i: (0, i)),
        ],
        out_specs=pl.BlockSpec((devices, tile // LANES, LANES), lambda i: (0, i, 0)),
        out_shape=jax.ShapeDtypeStruct((devices, columns // LANES, LANES), F32),
    )(mine, out_proj)
    partial = lax.all_to_all(partial, AXIS, split_axis=0, concat_axis=0, tiled=True)
    mixed = pl.pallas_call(
        sum_kernel,
        name="total",
        out_shape=jax.ShapeDtypeStruct((1, columns), BF16),
    )(partial)
    return (mixed, new_state[None])


def solution(mesh):
    in_specs = (
        P(("groups", "dp"), None, None, None),
        P(("groups", "dp"), None),
        P(("groups", "dp"), None),
        P(("groups", "dp"), None),
        P(("groups", "dp"), None),
        P(("groups", "dp"), None),
        P(),
        P(),
        P(),
        P(),
        P("dp", None),
        P(("groups", "dp")),
        P("groups", None),
    )
    out_specs = (P(("groups", "dp"), None), P(("groups", "dp"), None, None, None))
    return jax.shard_map(local, mesh=mesh, in_specs=in_specs, out_specs=out_specs, check_vma=False)
```

```python
import functools

import jax
import jax.numpy as jnp
from jax import lax
from jax.experimental import pallas as pl
from jax.experimental.pallas import tpu as pltpu
from jax.sharding import PartitionSpec as P

AXIS = "dp"
LANES = 128
MOST_PATTERNS = 32
GRANT = 8 * 2**20
F32 = jnp.float32
BF16 = jnp.bfloat16


def pair_switch(index, devices, array, beside, operands):
    def branch(distance, low_sends):
        pairs = [(i, i ^ distance) for i in range(devices) if (i < (i ^ distance)) == low_sends]
        return lambda a, ops: (lax.ppermute(a, AXIS, pairs), beside(*ops))

    branches = [branch(d, low) for d in range(1, devices) for low in (True, False)]
    return lax.switch(index, branches, array, operands)


def index_kernel(me, plan, index, live):
    def move(k, found):
        partner, sends = found
        source, target = plan[0, k], plan[1, k]
        partner = jnp.where(source == me[0], target, jnp.where(target == me[0], source, partner))
        return partner, jnp.where(source == me[0], 1, sends)

    partner, sends = lax.fori_loop(0, plan.shape[1], move, (jnp.int32(0), jnp.int32(0)))
    low_sends = jnp.where(me[0] < partner, sends, 1 - sends)
    index[0] = 2 * (jnp.bitwise_xor(me[0], partner) - 1) + 1 - low_sends
    live[0] = 1 - sends


def spread_and_collect(state, source, target, devices):
    ids = jnp.arange(devices, dtype=jnp.int32)
    matches = target[:, None] == ids[None, :]
    sender_of = jnp.sum(jnp.where(matches, source[:, None], 0), axis=0)
    has_sender = jnp.any(matches, axis=0)
    view = lax.all_to_all(state, AXIS, split_axis=1, concat_axis=0, tiled=True)
    routed = jnp.where(
        has_sender[:, None, None, None], jnp.take(view, sender_of, axis=0), jnp.zeros((), state.dtype)
    )
    return lax.all_to_all(routed, AXIS, split_axis=0, concat_axis=1, tiled=True)


def mix_kernel(live, s, x, z, b, c, per_head, gain, w, out, held_w, sem):
    copy = pltpu.make_async_copy(w, held_w, sem)
    copy.start()
    heads, p_size, n = s.shape
    groups = b.shape[1] // n
    held = heads // groups
    width = held * p_size
    for g in range(groups):
        at = slice(g * width, (g + 1) * width)
        bg, cg = b[:, g * n : (g + 1) * n], c[:, g * n : (g + 1) * n]
        t = lax.dot_general(
            jnp.broadcast_to(cg, (16, n)),
            s[g * held : (g + 1) * held].reshape(width, n),
            (((1,), (1,)), ((), ())),
            preferred_element_type=F32,
        )[0:1]
        bc = jnp.sum(bg.astype(F32) * cg.astype(F32), axis=1, keepdims=True)
        xf = x[:, at].astype(F32)
        y = per_head[0:1, at] * t + (per_head[1:2, at] * xf) * bc + per_head[2:3, at] * xf
        gated = y * jax.nn.silu(z[:, at].astype(F32))
        factor = lax.rsqrt(jnp.mean(gated * gated, axis=1, keepdims=True) + 1e-05)
        normed = jnp.where(live[0] > 0, gated * factor * gain[:, at], 0.0).astype(BF16)
        for q in range(width // LANES):
            row = g * (width // LANES) + q
            out[row : row + 1, :] = normed[:, q * LANES : (q + 1) * LANES]
    copy.wait()


def update_kernel(live, decay, s, x, b, per_head, out):
    heads, p_size, n = out.shape
    g = pl.program_id(0)
    dx = per_head[1:2] * x[...].astype(F32)
    first = dx.astype(BF16)
    rest = dx - first.astype(F32)
    second = rest.astype(BF16)
    third = (rest - second.astype(F32)).astype(BF16)
    row = lax.broadcasted_iota(jnp.int32, (16, dx.shape[1]), 0)
    terms = jnp.where(
        row == 0,
        first.astype(F32),
        jnp.where(row == 1, second.astype(F32), jnp.where(row == 2, third.astype(F32), 0.0)),
    ).astype(BF16)
    outer = lax.dot_general(
        terms, jnp.broadcast_to(b[...], (16, n)), (((0,), (0,)), ((), ())), preferred_element_type=F32
    )
    for h in range(heads):
        at = g * heads + h
        fresh = decay[at] * s[at].astype(F32) + outer[h * p_size : (h + 1) * p_size]
        out[h] = jnp.where(live[0] > 0, fresh, 0.0).astype(BF16)


def project_kernel(rows, w, out):
    tile = out.shape[1] * LANES
    lhs = jnp.concatenate([rows[:, r, :] for r in range(rows.shape[1])], axis=1)
    at = pl.ds(pl.multiple_of(pl.program_id(0) * tile, tile), tile)
    total = jnp.dot(lhs, w[:, at], preferred_element_type=F32).astype(out.dtype)
    for j in range(tile // LANES):
        out[:, j, :] = total[:, j * LANES : (j + 1) * LANES]


def sum_kernel(parts, out):
    total = jnp.sum(parts[...].astype(F32), axis=0).astype(BF16)
    for q in range(total.shape[0]):
        out[0:1, q * LANES : (q + 1) * LANES] = total[q : q + 1, :]


def local(
    state,
    x_in,
    z_gate,
    b_in,
    c_in,
    dt_raw,
    dt_bias,
    a_log,
    d_skip,
    norm_gain,
    out_proj,
    active,
    plan,
):
    devices = lax.axis_size(AXIS)
    me = lax.axis_index(AXIS)
    heads, p_size, n = state.shape[1:]
    groups = b_in.shape[1] // n
    width = heads * p_size
    columns = out_proj.shape[1]
    source, target = plan[:, 0], plan[:, 1]
    smem = pl.BlockSpec(memory_space=pltpu.SMEM)
    index, live = pl.pallas_call(
        index_kernel,
        name="index",
        in_specs=[smem, smem],
        out_specs=(smem, smem),
        out_shape=(jax.ShapeDtypeStruct((1,), jnp.int32),) * 2,
    )(me.astype(jnp.int32).reshape(1), plan.T)

    def prepare(dt_raw, dt_bias, a_log, d_skip):
        step = jax.nn.softplus(dt_raw[0] + dt_bias)
        decay = jnp.exp(-jnp.exp(a_log) * step)
        return decay, jnp.repeat(jnp.stack([decay, step, d_skip]), p_size, axis=1)

    operands = (dt_raw, dt_bias, a_log, d_skip)

    if 2 * (devices - 1) <= MOST_PATTERNS and devices & (devices - 1) == 0:
        came, (decay, per_head) = pair_switch(index[0], devices, state, prepare, operands)
    else:
        came = spread_and_collect(state, source, target, devices)
        decay, per_head = prepare(*operands)
    came = came.reshape(heads, p_size, n)
    gain = norm_gain.reshape(1, width)

    of_group = width // groups
    row_spec = pl.BlockSpec((1, of_group), lambda g: (0, g))
    vmem = pl.BlockSpec(memory_space=pltpu.VMEM)
    in_vmem = functools.partial(pltpu.with_memory_space_constraint, memory_space=pltpu.VMEM)
    params = pltpu.CompilerParams(vmem_limit_bytes=GRANT)
    came = in_vmem(came)

    normed, weights = pl.pallas_call(
        mix_kernel,
        name="mix",
        in_specs=[smem] + [vmem] * 7 + [pl.BlockSpec(memory_space=pltpu.HBM)],
        out_specs=(vmem, vmem),
        out_shape=(
            jax.ShapeDtypeStruct((width // LANES, LANES), BF16),
            pltpu.VMEM(out_proj.shape, BF16),
        ),
        scratch_shapes=[pltpu.SemaphoreType.DMA],
        compiler_params=params,
    )(live, came, *[in_vmem(a) for a in (x_in, z_gate, b_in, c_in, per_head, gain)], pltpu.with_memory_space_constraint(out_proj, pltpu.HBM))

    block = width // devices
    lanes = min(block, LANES)
    mine = lax.all_to_all(
        normed.reshape(devices, block // lanes, lanes), AXIS, split_axis=0, concat_axis=0, tiled=True
    )

    new_state = pl.pallas_call(
        update_kernel,
        name="update",
        grid=(groups,),
        in_specs=[
            smem,
            smem,
            vmem,
            row_spec,
            pl.BlockSpec((1, n), lambda g: (0, g)),
            pl.BlockSpec((3, of_group), lambda g: (0, g)),
        ],
        out_specs=pl.BlockSpec((heads // groups, p_size, n), lambda g: (g, 0, 0)),
        out_shape=jax.ShapeDtypeStruct((heads, p_size, n), BF16),
        compiler_params=params,
    )(live, decay, came, x_in, b_in, per_head)

    tile = 1024
    partial = pl.pallas_call(
        project_kernel,
        name="project",
        grid=(columns // tile,),
        in_specs=[vmem, vmem],
        out_specs=pl.BlockSpec((devices, tile // LANES, LANES), lambda i: (0, i, 0)),
        out_shape=jax.ShapeDtypeStruct((devices, columns // LANES, LANES), BF16),
        compiler_params=params,
    )(in_vmem(mine), in_vmem(weights))
    partial = lax.all_to_all(partial, AXIS, split_axis=0, concat_axis=0, tiled=True)
    mixed = pl.pallas_call(
        sum_kernel,
        name="total",
        in_specs=[vmem],
        out_shape=jax.ShapeDtypeStruct((1, columns), BF16),
        compiler_params=params,
    )(in_vmem(partial))
    return (mixed, new_state[None])


def solution(mesh):
    in_specs = (
        P(("groups", "dp"), None, None, None),
        P(("groups", "dp"), None),
        P(("groups", "dp"), None),
        P(("groups", "dp"), None),
        P(("groups", "dp"), None),
        P(("groups", "dp"), None),
        P(),
        P(),
        P(),
        P(),
        P("dp", None),
        P(("groups", "dp")),
        P("groups", None),
    )
    out_specs = (P(("groups", "dp"), None), P(("groups", "dp"), None, None, None))
    return jax.shard_map(local, mesh=mesh, in_specs=in_specs, out_specs=out_specs, check_vma=False)
```

```python
import functools

import jax
import jax.numpy as jnp
from jax import lax
from jax.experimental import pallas as pl
from jax.experimental.pallas import tpu as pltpu
from jax.sharding import PartitionSpec as P

AXIS = "dp"
LANES = 128
MOST_PATTERNS = 32
TILE = 1024
FIRST = 2
GRANT = 16 * 2**20
F32 = jnp.float32
BF16 = jnp.bfloat16


def pair_switch(index, devices, array, beside, operands):
    def branch(distance, low_sends):
        pairs = [(i, i ^ distance) for i in range(devices) if (i < (i ^ distance)) == low_sends]
        return lambda a, ops: (lax.ppermute(a, AXIS, pairs), beside(*ops))

    branches = [branch(d, low) for d in range(1, devices) for low in (True, False)]
    return lax.switch(index, branches, array, operands)


def index_kernel(me, plan, index, live):
    def move(k, found):
        partner, sends = found
        source, target = plan[0, k], plan[1, k]
        partner = jnp.where(source == me[0], target, jnp.where(target == me[0], source, partner))
        return partner, jnp.where(source == me[0], 1, sends)

    partner, sends = lax.fori_loop(0, plan.shape[1], move, (jnp.int32(0), jnp.int32(0)))
    low_sends = jnp.where(me[0] < partner, sends, 1 - sends)
    index[0] = 2 * (jnp.bitwise_xor(me[0], partner) - 1) + 1 - low_sends
    live[0] = 1 - sends


def spread_and_collect(state, source, target, devices):
    ids = jnp.arange(devices, dtype=jnp.int32)
    matches = target[:, None] == ids[None, :]
    sender_of = jnp.sum(jnp.where(matches, source[:, None], 0), axis=0)
    has_sender = jnp.any(matches, axis=0)
    view = lax.all_to_all(state, AXIS, split_axis=1, concat_axis=0, tiled=True)
    routed = jnp.where(
        has_sender[:, None, None, None], jnp.take(view, sender_of, axis=0), jnp.zeros((), state.dtype)
    )
    return lax.all_to_all(routed, AXIS, split_axis=0, concat_axis=1, tiled=True)


def mix_kernel(live, s, x, z, b, c, per_head, gain, w, out, first_w, state, sems):
    groups = b.shape[1] // s.shape[2]
    held = s.shape[0] // groups
    p_size, n = s.shape[1:]
    width = held * p_size
    copies = [
        pltpu.make_async_copy(s.at[pl.ds(g * held, held)], state.at[pl.ds(g * held, held)], sems.at[g])
        for g in range(groups)
    ]
    copies.append(pltpu.make_async_copy(w.at[:, pl.ds(0, first_w.shape[1])], first_w, sems.at[groups]))
    for copy in copies:
        copy.start()
    for g in range(groups):
        at = slice(g * width, (g + 1) * width)
        bg, cg = b[:, g * n : (g + 1) * n], c[:, g * n : (g + 1) * n]
        bc = jnp.sum(bg.astype(F32) * cg.astype(F32), axis=1, keepdims=True)
        xf = x[:, at].astype(F32)
        rest = (per_head[1:2, at] * xf) * bc + per_head[2:3, at] * xf
        gate = jax.nn.silu(z[:, at].astype(F32))
        copies[g].wait()
        t = lax.dot_general(
            jnp.broadcast_to(cg, (16, n)),
            state[g * held : (g + 1) * held].reshape(width, n),
            (((1,), (1,)), ((), ())),
            preferred_element_type=F32,
        )[0:1]
        gated = (per_head[0:1, at] * t + rest) * gate
        factor = lax.rsqrt(jnp.mean(gated * gated, axis=1, keepdims=True) + 1e-05)
        normed = jnp.where(live[0] > 0, gated * factor * gain[:, at], 0.0).astype(BF16)
        for q in range(width // LANES):
            row = g * (width // LANES) + q
            out[row : row + 1, :] = normed[:, q * LANES : (q + 1) * LANES]
    copies[groups].wait()


def update_kernel(live, decay, s, x, b, per_head, out):
    heads, p_size, n = out.shape
    g = pl.program_id(0)
    dx = per_head[1:2] * x[...].astype(F32)
    first = dx.astype(BF16)
    rest = dx - first.astype(F32)
    second = rest.astype(BF16)
    third = (rest - second.astype(F32)).astype(BF16)
    row = lax.broadcasted_iota(jnp.int32, (16, dx.shape[1]), 0)
    terms = jnp.where(
        row == 0,
        first.astype(F32),
        jnp.where(row == 1, second.astype(F32), jnp.where(row == 2, third.astype(F32), 0.0)),
    ).astype(BF16)
    outer = lax.dot_general(
        terms, jnp.broadcast_to(b[...], (16, n)), (((0,), (0,)), ((), ())), preferred_element_type=F32
    )
    for h in range(heads):
        fresh = decay[g * heads + h] * s[h].astype(F32) + outer[h * p_size : (h + 1) * p_size]
        out[h] = jnp.where(live[0] > 0, fresh, 0.0).astype(BF16)


def project_kernel(rows, first_w, w, out, rest_w, sems):
    tiles = w.shape[1] // TILE
    have = first_w.shape[1] // TILE
    copies = [
        pltpu.make_async_copy(
            w.at[:, pl.ds((have + i) * TILE, TILE)], rest_w.at[:, pl.ds(i * TILE, TILE)], sems.at[i]
        )
        for i in range(tiles - have)
    ]
    for copy in copies:
        copy.start()
    lhs = jnp.concatenate([rows[:, r, :] for r in range(rows.shape[1])], axis=1)
    for i in range(tiles):
        if i < have:
            weights = first_w[:, i * TILE : (i + 1) * TILE]
        else:
            copies[i - have].wait()
            weights = rest_w[:, (i - have) * TILE : (i - have + 1) * TILE]
        total = jnp.dot(lhs, weights, preferred_element_type=F32).astype(out.dtype)
        for j in range(TILE // LANES):
            out[:, i * (TILE // LANES) + j, :] = total[:, j * LANES : (j + 1) * LANES]


def sum_kernel(parts, out):
    total = jnp.sum(parts[...].astype(F32), axis=0).astype(BF16)
    for q in range(total.shape[0]):
        out[0:1, q * LANES : (q + 1) * LANES] = total[q : q + 1, :]


def local(
    state,
    x_in,
    z_gate,
    b_in,
    c_in,
    dt_raw,
    dt_bias,
    a_log,
    d_skip,
    norm_gain,
    out_proj,
    active,
    plan,
):
    devices = lax.axis_size(AXIS)
    me = lax.axis_index(AXIS)
    heads, p_size, n = state.shape[1:]
    groups = b_in.shape[1] // n
    width = heads * p_size
    columns = out_proj.shape[1]
    source, target = plan[:, 0], plan[:, 1]
    smem = pl.BlockSpec(memory_space=pltpu.SMEM)
    index, live = pl.pallas_call(
        index_kernel,
        name="index",
        in_specs=[smem, smem],
        out_specs=(smem, smem),
        out_shape=(jax.ShapeDtypeStruct((1,), jnp.int32),) * 2,
    )(me.astype(jnp.int32).reshape(1), plan.T)

    def prepare(dt_raw, dt_bias, a_log, d_skip):
        step = jax.nn.softplus(dt_raw[0] + dt_bias)
        decay = jnp.exp(-jnp.exp(a_log) * step)
        return decay, jnp.repeat(jnp.stack([decay, step, d_skip]), p_size, axis=1)

    operands = (dt_raw, dt_bias, a_log, d_skip)

    if 2 * (devices - 1) <= MOST_PATTERNS and devices & (devices - 1) == 0:
        came, (decay, per_head) = pair_switch(index[0], devices, state, prepare, operands)
    else:
        came = spread_and_collect(state, source, target, devices)
        decay, per_head = prepare(*operands)
    came = came.reshape(heads, p_size, n)
    gain = norm_gain.reshape(1, width)

    of_group = width // groups
    row_spec = pl.BlockSpec((1, of_group), lambda g: (0, g))
    vmem = pl.BlockSpec(memory_space=pltpu.VMEM)
    in_vmem = functools.partial(pltpu.with_memory_space_constraint, memory_space=pltpu.VMEM)
    params = pltpu.CompilerParams(vmem_limit_bytes=GRANT)
    in_hbm = functools.partial(pltpu.with_memory_space_constraint, memory_space=pltpu.HBM)
    hbm = pl.BlockSpec(memory_space=pltpu.HBM)
    weights = in_hbm(out_proj)

    normed, first_w = pl.pallas_call(
        mix_kernel,
        name="mix",
        in_specs=[smem, hbm] + [vmem] * 6 + [hbm],
        out_specs=(vmem, vmem),
        out_shape=(
            jax.ShapeDtypeStruct((width // LANES, LANES), BF16),
            pltpu.VMEM((out_proj.shape[0], FIRST * TILE), BF16),
        ),
        scratch_shapes=[
            pltpu.VMEM((heads, p_size, n), BF16),
            pltpu.SemaphoreType.DMA((groups + 1,)),
        ],
        compiler_params=params,
    )(
        live,
        in_hbm(came),
        *[in_vmem(a) for a in (x_in, z_gate, b_in, c_in, per_head, gain)],
        weights,
    )

    block = width // devices
    lanes = min(block, LANES)
    mine = lax.all_to_all(
        normed.reshape(devices, block // lanes, lanes), AXIS, split_axis=0, concat_axis=0, tiled=True
    )

    new_state = pl.pallas_call(
        update_kernel,
        name="update",
        grid=(groups,),
        in_specs=[
            smem,
            smem,
            pl.BlockSpec((heads // groups, p_size, n), lambda g: (g, 0, 0)),
            row_spec,
            pl.BlockSpec((1, n), lambda g: (0, g)),
            pl.BlockSpec((3, of_group), lambda g: (0, g)),
        ],
        out_specs=pl.BlockSpec((heads // groups, p_size, n), lambda g: (g, 0, 0)),
        out_shape=jax.ShapeDtypeStruct((heads, p_size, n), BF16),
        compiler_params=params,
    )(live, decay, came, x_in, b_in, per_head)

    partial = pl.pallas_call(
        project_kernel,
        name="project",
        in_specs=[vmem, vmem, hbm],
        out_specs=vmem,
        out_shape=jax.ShapeDtypeStruct((devices, columns // LANES, LANES), BF16),
        scratch_shapes=[
            pltpu.VMEM((out_proj.shape[0], columns - FIRST * TILE), BF16),
            pltpu.SemaphoreType.DMA((columns // TILE - FIRST,)),
        ],
        compiler_params=params,
    )(in_vmem(mine), in_vmem(first_w), weights)
    partial = lax.all_to_all(partial, AXIS, split_axis=0, concat_axis=0, tiled=True)
    mixed = pl.pallas_call(
        sum_kernel,
        name="total",
        in_specs=[vmem],
        out_shape=jax.ShapeDtypeStruct((1, columns), BF16),
        compiler_params=params,
    )(in_vmem(partial))
    return (mixed, new_state[None])


def solution(mesh):
    in_specs = (
        P(("groups", "dp"), None, None, None),
        P(("groups", "dp"), None),
        P(("groups", "dp"), None),
        P(("groups", "dp"), None),
        P(("groups", "dp"), None),
        P(("groups", "dp"), None),
        P(),
        P(),
        P(),
        P(),
        P("dp", None),
        P(("groups", "dp")),
        P("groups", None),
    )
    out_specs = (P(("groups", "dp"), None), P(("groups", "dp"), None, None, None))
    return jax.shard_map(local, mesh=mesh, in_specs=in_specs, out_specs=out_specs, check_vma=False)
```

```python
import functools

import jax
import jax.numpy as jnp
from jax import lax
from jax.experimental import pallas as pl
from jax.experimental.pallas import tpu as pltpu
from jax.sharding import PartitionSpec as P

AXIS = "dp"
LANES = 128
MOST_PATTERNS = 32
TILE = 1024
FIRST = 2
GRANT = 16 * 2**20
F32 = jnp.float32
BF16 = jnp.bfloat16


def pair_switch(index, devices, state, rows_of, beside, operands):
    def branch(distance, low_sends):
        pairs = [(i, i ^ distance) for i in range(devices) if (i < (i ^ distance)) == low_sends]
        back = [(t, s) for s, t in pairs]

        def move(state, operands):
            came = lax.ppermute(state, AXIS, pairs)
            theirs = lax.ppermute(rows_of(*operands), AXIS, back)
            return came, beside(theirs, state, *operands)

        return move

    branches = [branch(d, low) for d in range(1, devices) for low in (True, False)]
    return lax.switch(index, branches, state, operands)


def index_kernel(me, plan, index, live):
    def move(k, found):
        partner, sends = found
        source, target = plan[0, k], plan[1, k]
        partner = jnp.where(source == me[0], target, jnp.where(target == me[0], source, partner))
        return partner, jnp.where(source == me[0], 1, sends)

    partner, sends = lax.fori_loop(0, plan.shape[1], move, (jnp.int32(0), jnp.int32(0)))
    low_sends = jnp.where(me[0] < partner, sends, 1 - sends)
    index[0] = 2 * (jnp.bitwise_xor(me[0], partner) - 1) + 1 - low_sends
    live[0] = 1 - sends


def spread_and_collect(state, source, target, devices):
    ids = jnp.arange(devices, dtype=jnp.int32)
    matches = target[:, None] == ids[None, :]
    sender_of = jnp.sum(jnp.where(matches, source[:, None], 0), axis=0)
    has_sender = jnp.any(matches, axis=0)
    view = lax.all_to_all(state, AXIS, split_axis=1, concat_axis=0, tiled=True)
    routed = jnp.where(
        has_sender[:, None, None, None], jnp.take(view, sender_of, axis=0), jnp.zeros((), state.dtype)
    )
    return lax.all_to_all(routed, AXIS, split_axis=0, concat_axis=1, tiled=True)


def split(value):
    first = value.astype(BF16).astype(F32)
    second = (value - first).astype(BF16).astype(F32)
    return first, second, value - first - second


def pack_kernel(x, z, b, c, dt, out):
    first, second, third = split(dt[...])
    upper = [x[...].astype(F32), b[...].astype(F32), first, second]
    lower = [z[...].astype(F32), c[...].astype(F32), third, jnp.zeros_like(third)]
    at = 0
    for up, low in zip(upper, lower):
        width = up.shape[1]
        shape = (2, width)
        row = lax.broadcasted_iota(jnp.int32, shape, 0)
        both = jnp.where(row == 0, jnp.broadcast_to(up, shape), jnp.broadcast_to(low, shape))
        out[:, at : at + width] = both.astype(BF16)
        at += width


def mix_kernel(s, xz, bc, per_head, gain, out):
    heads, p_size, n = s.shape
    rows = bc[...].astype(F32)
    b, c = rows[0:1], rows[1:2]
    t = lax.dot_general(
        jnp.broadcast_to(c, (16, n)).astype(BF16),
        s[...].reshape(heads * p_size, n),
        (((1,), (1,)), ((), ())),
        preferred_element_type=F32,
    )[0:1]
    both = xz[...].astype(F32)
    x, z = both[0:1], both[1:2]
    y = (
        per_head[0:1] * t
        + (per_head[1:2] * x) * jnp.sum(b * c, axis=1, keepdims=True)
        + per_head[2:3] * x
    )
    gated = y * jax.nn.silu(z)
    factor = lax.rsqrt(jnp.mean(gated * gated, axis=1, keepdims=True) + 1e-05)
    normed = (gated * factor * gain[...]).astype(BF16)
    for q in range(normed.shape[1] // LANES):
        out[q : q + 1, :] = normed[:, q * LANES : (q + 1) * LANES]


def hold_kernel(moves, w, out, takes, sem):
    copy = pltpu.make_async_copy(w.at[:, pl.ds(0, out.shape[1])], out, sem)
    copy.start()
    to = lax.broadcasted_iota(jnp.int32, takes.shape, 0)
    of = lax.broadcasted_iota(jnp.int32, takes.shape, 1)

    def add(k, found):
        return jnp.where((of == moves[0, k]) & (to == moves[1, k]), 1.0, found)

    found = lax.fori_loop(0, moves.shape[1], add, jnp.zeros(takes.shape, F32))
    takes[...] = found.astype(BF16)
    copy.wait()


def update_kernel(live, decay, s, x, b, step, out):
    heads, p_size, n = out.shape
    g = pl.program_id(0)
    dx = step[...] * x[...].astype(F32)
    first, second, third = split(dx)
    row = lax.broadcasted_iota(jnp.int32, (16, dx.shape[1]), 0)
    terms = jnp.where(
        row == 0, first, jnp.where(row == 1, second, jnp.where(row == 2, third, 0.0))
    ).astype(BF16)
    outer = lax.dot_general(
        terms, jnp.broadcast_to(b[...], (16, n)), (((0,), (0,)), ((), ())), preferred_element_type=F32
    )
    for h in range(heads):
        fresh = decay[g * heads + h] * s[h].astype(F32) + outer[h * p_size : (h + 1) * p_size]
        out[h] = jnp.where(live[0] > 0, fresh, 0.0).astype(BF16)


def project_kernel(takes, rows, first_w, w, out, rest_w, sems):
    tiles = w.shape[1] // TILE
    have = first_w.shape[1] // TILE
    copies = [
        pltpu.make_async_copy(
            w.at[:, pl.ds((have + i) * TILE, TILE)], rest_w.at[:, pl.ds(i * TILE, TILE)], sems.at[i]
        )
        for i in range(tiles - have)
    ]
    for copy in copies:
        copy.start()
    lhs = jnp.concatenate([rows[:, r, :] for r in range(rows.shape[1])], axis=1)
    lhs = jnp.dot(takes[...], lhs, preferred_element_type=F32).astype(BF16)
    for i in range(tiles):
        if i < have:
            weights = first_w[:, i * TILE : (i + 1) * TILE]
        else:
            copies[i - have].wait()
            weights = rest_w[:, (i - have) * TILE : (i - have + 1) * TILE]
        total = jnp.dot(lhs, weights, preferred_element_type=F32).astype(out.dtype)
        for j in range(TILE // LANES):
            out[:, i * (TILE // LANES) + j, :] = total[:, j * LANES : (j + 1) * LANES]


def sum_kernel(parts, out):
    total = jnp.sum(parts[...].astype(F32), axis=0).astype(BF16)
    for q in range(total.shape[0]):
        out[0:1, q * LANES : (q + 1) * LANES] = total[q : q + 1, :]


def local(
    state,
    x_in,
    z_gate,
    b_in,
    c_in,
    dt_raw,
    dt_bias,
    a_log,
    d_skip,
    norm_gain,
    out_proj,
    active,
    plan,
):
    devices = lax.axis_size(AXIS)
    me = lax.axis_index(AXIS)
    heads, p_size, n = state.shape[1:]
    groups = b_in.shape[1] // n
    width = heads * p_size
    columns = out_proj.shape[1]
    source, target = plan[:, 0], plan[:, 1]
    smem = pl.BlockSpec(memory_space=pltpu.SMEM)
    index, live = pl.pallas_call(
        index_kernel,
        name="index",
        in_specs=[smem, smem],
        out_specs=(smem, smem),
        out_shape=(jax.ShapeDtypeStruct((1,), jnp.int32),) * 2,
    )(me.astype(jnp.int32).reshape(1), plan.T)

    of_group = width // groups
    vmem = pl.BlockSpec(memory_space=pltpu.VMEM)
    hbm = pl.BlockSpec(memory_space=pltpu.HBM)
    in_vmem = functools.partial(pltpu.with_memory_space_constraint, memory_space=pltpu.VMEM)
    params = pltpu.CompilerParams(vmem_limit_bytes=GRANT)
    state_spec = pl.BlockSpec((heads // groups, p_size, n), lambda g: (g, 0, 0))
    row_spec = pl.BlockSpec((1, of_group), lambda g: (0, g))
    weights = pltpu.with_memory_space_constraint(out_proj, pltpu.HBM)
    gain = norm_gain.reshape(1, width)

    def rows_of(x_in, z_gate, b_in, c_in, dt_raw, *_):
        return pl.pallas_call(
            pack_kernel,
            name="pack",
            out_shape=jax.ShapeDtypeStruct((2, width + groups * n + 2 * heads), BF16),
            compiler_params=params,
        )(x_in, z_gate, b_in, c_in, dt_raw)

    def beside(
        theirs, state, x_in, z_gate, b_in, c_in, dt_raw, dt_bias, a_log, d_skip, gain, weights, moves
    ):
        ends = theirs[:, width + groups * n :].astype(F32)
        their_dt = (ends[0, :heads] + ends[0, heads:]) + ends[1, :heads]
        step = jax.nn.softplus(jnp.stack([their_dt, dt_raw[0]]) + dt_bias)
        decay = jnp.exp(-jnp.exp(a_log) * step)
        each = jnp.stack([decay[0], step[0], d_skip, step[1]])
        per_head = jnp.repeat(each, p_size, axis=1)
        normed = pl.pallas_call(
            mix_kernel,
            name="mix",
            grid=(groups,),
            in_specs=[
                state_spec,
                pl.BlockSpec((2, of_group), lambda g: (0, g)),
                pl.BlockSpec((2, n), lambda g: (0, width // n + g)),
                pl.BlockSpec((4, of_group), lambda g: (0, g)),
                row_spec,
            ],
            out_specs=pl.BlockSpec((of_group // LANES, LANES), lambda g: (g, 0)),
            out_shape=jax.ShapeDtypeStruct((width // LANES, LANES), BF16),
            compiler_params=params,
        )(state.reshape(heads, p_size, n), theirs, theirs, per_head, gain)
        first_w, takes = pl.pallas_call(
            hold_kernel,
            name="hold",
            in_specs=[smem, hbm],
            out_specs=(vmem, vmem),
            out_shape=(
                pltpu.VMEM((weights.shape[0], FIRST * TILE), BF16),
                pltpu.VMEM((devices, devices), BF16),
            ),
            scratch_shapes=[pltpu.SemaphoreType.DMA],
            compiler_params=params,
        )(moves, pltpu.with_memory_space_constraint(weights, pltpu.HBM))
        return normed, first_w, takes, decay[1], per_head[3:4]

    operands = (x_in, z_gate, b_in, c_in, dt_raw, dt_bias, a_log, d_skip, gain, out_proj)
    if 2 * (devices - 1) <= MOST_PATTERNS and devices & (devices - 1) == 0:
        came, (normed, first_w, takes, decay, step) = pair_switch(
            index[0], devices, state, rows_of, beside, operands + (plan.T,)
        )
    else:
        came = spread_and_collect(state, source, target, devices)
        own = jnp.stack([target, target])
        normed, first_w, takes, decay, step = beside(rows_of(*operands), came, *operands, own)
    came = came.reshape(heads, p_size, n)

    block = width // devices
    lanes = min(block, LANES)
    mine = lax.all_to_all(
        normed.reshape(devices, block // lanes, lanes), AXIS, split_axis=0, concat_axis=0, tiled=True
    )

    new_state = pl.pallas_call(
        update_kernel,
        name="update",
        grid=(groups,),
        in_specs=[smem, smem, state_spec, row_spec, pl.BlockSpec((1, n), lambda g: (0, g)), row_spec],
        out_specs=state_spec,
        out_shape=jax.ShapeDtypeStruct((heads, p_size, n), BF16),
        compiler_params=params,
    )(live, decay, came, x_in, b_in, step)

    partial = pl.pallas_call(
        project_kernel,
        name="project",
        in_specs=[vmem, vmem, vmem, hbm],
        out_specs=vmem,
        out_shape=jax.ShapeDtypeStruct((devices, columns // LANES, LANES), BF16),
        scratch_shapes=[
            pltpu.VMEM((out_proj.shape[0], columns - FIRST * TILE), BF16),
            pltpu.SemaphoreType.DMA((columns // TILE - FIRST,)),
        ],
        compiler_params=params,
    )(in_vmem(takes), in_vmem(mine), in_vmem(first_w), weights)
    partial = lax.all_to_all(partial, AXIS, split_axis=0, concat_axis=0, tiled=True)
    mixed = pl.pallas_call(
        sum_kernel,
        name="total",
        in_specs=[vmem],
        out_shape=jax.ShapeDtypeStruct((1, columns), BF16),
        compiler_params=params,
    )(in_vmem(partial))
    return (mixed, new_state[None])


def solution(mesh):
    in_specs = (
        P(("groups", "dp"), None, None, None),
        P(("groups", "dp"), None),
        P(("groups", "dp"), None),
        P(("groups", "dp"), None),
        P(("groups", "dp"), None),
        P(("groups", "dp"), None),
        P(),
        P(),
        P(),
        P(),
        P("dp", None),
        P(("groups", "dp")),
        P("groups", None),
    )
    out_specs = (P(("groups", "dp"), None), P(("groups", "dp"), None, None, None))
    return jax.shard_map(local, mesh=mesh, in_specs=in_specs, out_specs=out_specs, check_vma=False)
```

```python
import functools

import jax
import jax.numpy as jnp
from jax import lax
from jax.experimental import pallas as pl
from jax.experimental.pallas import tpu as pltpu
from jax.sharding import PartitionSpec as P

AXIS = "dp"
LANES = 128
MOST_PATTERNS = 32
TILE = 1024
FIRST = 2
GRANT = 16 * 2**20
F32 = jnp.float32
BF16 = jnp.bfloat16


def pair_switch(index, devices, state, rows_of, beside, operands):
    def branch(distance, low_sends):
        pairs = [(i, i ^ distance) for i in range(devices) if (i < (i ^ distance)) == low_sends]
        back = [(t, s) for s, t in pairs]

        def move(state, operands):
            came = lax.ppermute(state, AXIS, pairs)
            theirs = lax.ppermute(rows_of(*operands), AXIS, back)
            return came, beside(theirs, state, *operands)

        return move

    branches = [branch(d, low) for d in range(1, devices) for low in (True, False)]
    return lax.switch(index, branches, state, operands)


def index_kernel(me, plan, index, live):
    def move(k, found):
        partner, sends = found
        source, target = plan[0, k], plan[1, k]
        partner = jnp.where(source == me[0], target, jnp.where(target == me[0], source, partner))
        return partner, jnp.where(source == me[0], 1, sends)

    partner, sends = lax.fori_loop(0, plan.shape[1], move, (jnp.int32(0), jnp.int32(0)))
    low_sends = jnp.where(me[0] < partner, sends, 1 - sends)
    index[0] = 2 * (jnp.bitwise_xor(me[0], partner) - 1) + 1 - low_sends
    live[0] = 1 - sends


def spread_and_collect(state, source, target, devices):
    ids = jnp.arange(devices, dtype=jnp.int32)
    matches = target[:, None] == ids[None, :]
    sender_of = jnp.sum(jnp.where(matches, source[:, None], 0), axis=0)
    has_sender = jnp.any(matches, axis=0)
    view = lax.all_to_all(state, AXIS, split_axis=1, concat_axis=0, tiled=True)
    routed = jnp.where(
        has_sender[:, None, None, None], jnp.take(view, sender_of, axis=0), jnp.zeros((), state.dtype)
    )
    return lax.all_to_all(routed, AXIS, split_axis=0, concat_axis=1, tiled=True)


def split(value):
    first = value.astype(BF16).astype(F32)
    second = (value - first).astype(BF16).astype(F32)
    return first, second, value - first - second


def pack_kernel(x, z, b, c, dt, out):
    first, second, third = split(dt[...])
    upper = [x[...].astype(F32), b[...].astype(F32), first, second]
    lower = [z[...].astype(F32), c[...].astype(F32), third, jnp.zeros_like(third)]
    at = 0
    for up, low in zip(upper, lower):
        width = up.shape[1]
        shape = (2, width)
        row = lax.broadcasted_iota(jnp.int32, shape, 0)
        both = jnp.where(row == 0, jnp.broadcast_to(up, shape), jnp.broadcast_to(low, shape))
        out[:, at : at + width] = both.astype(BF16)
        at += width


def mix_kernel(s, xz, bc, per_head, gain, out):
    heads, p_size, n = s.shape
    rows = bc[...].astype(F32)
    b, c = rows[0:1], rows[1:2]
    t = lax.dot_general(
        jnp.broadcast_to(c, (16, n)).astype(BF16),
        s[...].reshape(heads * p_size, n),
        (((1,), (1,)), ((), ())),
        preferred_element_type=F32,
    )[0:1]
    both = xz[...].astype(F32)
    x, z = both[0:1], both[1:2]
    y = (
        per_head[0:1] * t
        + (per_head[1:2] * x) * jnp.sum(b * c, axis=1, keepdims=True)
        + per_head[2:3] * x
    )
    gated = y * jax.nn.silu(z)
    factor = lax.rsqrt(jnp.mean(gated * gated, axis=1, keepdims=True) + 1e-05)
    normed = (gated * factor * gain[...]).astype(BF16)
    for q in range(normed.shape[1] // LANES):
        out[q : q + 1, :] = normed[:, q * LANES : (q + 1) * LANES]


def hold_kernel(moves, w, out, takes, sem):
    copy = pltpu.make_async_copy(w.at[:, pl.ds(0, out.shape[1])], out, sem)
    copy.start()
    to = lax.broadcasted_iota(jnp.int32, takes.shape, 0)
    of = lax.broadcasted_iota(jnp.int32, takes.shape, 1)

    def add(k, found):
        return jnp.where((of == moves[0, k]) & (to == moves[1, k]), 1.0, found)

    found = lax.fori_loop(0, moves.shape[1], add, jnp.zeros(takes.shape, F32))
    takes[...] = found.astype(BF16)
    copy.wait()


def update_kernel(live, decay, s, x, b, step, out):
    heads, p_size, n = out.shape
    g = pl.program_id(0)
    dx = step[...] * x[...].astype(F32)
    first, second, third = split(dx)
    row = lax.broadcasted_iota(jnp.int32, (16, dx.shape[1]), 0)
    terms = jnp.where(
        row == 0, first, jnp.where(row == 1, second, jnp.where(row == 2, third, 0.0))
    ).astype(BF16)
    outer = lax.dot_general(
        terms, jnp.broadcast_to(b[...], (16, n)), (((0,), (0,)), ((), ())), preferred_element_type=F32
    )
    for h in range(heads):
        fresh = decay[g * heads + h] * s[h].astype(F32) + outer[h * p_size : (h + 1) * p_size]
        out[h] = jnp.where(live[0] > 0, fresh, 0.0).astype(BF16)


def project_kernel(takes, rows, first_w, w, out, rest_w, sems):
    tiles = w.shape[1] // TILE
    have = first_w.shape[1] // TILE
    copies = [
        pltpu.make_async_copy(
            w.at[:, pl.ds((have + i) * TILE, TILE)], rest_w.at[:, pl.ds(i * TILE, TILE)], sems.at[i]
        )
        for i in range(tiles - have)
    ]
    for copy in copies:
        copy.start()
    lhs = jnp.concatenate([rows[:, r, :] for r in range(rows.shape[1])], axis=1)
    lhs = jnp.dot(takes[...], lhs, preferred_element_type=F32).astype(BF16)
    for i in range(tiles):
        if i < have:
            weights = first_w[:, i * TILE : (i + 1) * TILE]
        else:
            copies[i - have].wait()
            weights = rest_w[:, (i - have) * TILE : (i - have + 1) * TILE]
        total = jnp.dot(lhs, weights, preferred_element_type=F32).astype(out.dtype)
        for j in range(TILE // LANES):
            out[:, i * (TILE // LANES) + j, :] = total[:, j * LANES : (j + 1) * LANES]


def sum_kernel(parts, out):
    total = jnp.sum(parts[...].astype(F32), axis=0).astype(BF16)
    for q in range(total.shape[0]):
        out[0:1, q * LANES : (q + 1) * LANES] = total[q : q + 1, :]


def local(
    state,
    x_in,
    z_gate,
    b_in,
    c_in,
    dt_raw,
    dt_bias,
    a_log,
    d_skip,
    norm_gain,
    out_proj,
    active,
    plan,
):
    devices = lax.axis_size(AXIS)
    me = lax.axis_index(AXIS)
    heads, p_size, n = state.shape[1:]
    groups = b_in.shape[1] // n
    width = heads * p_size
    columns = out_proj.shape[1]
    source, target = plan[:, 0], plan[:, 1]
    smem = pl.BlockSpec(memory_space=pltpu.SMEM)
    index, live = pl.pallas_call(
        index_kernel,
        name="index",
        in_specs=[smem, smem],
        out_specs=(smem, smem),
        out_shape=(pltpu.SMEM((1,), jnp.int32),) * 2,
    )(me.astype(jnp.int32).reshape(1), plan.T)

    of_group = width // groups
    vmem = pl.BlockSpec(memory_space=pltpu.VMEM)
    hbm = pl.BlockSpec(memory_space=pltpu.HBM)
    in_vmem = functools.partial(pltpu.with_memory_space_constraint, memory_space=pltpu.VMEM)
    params = pltpu.CompilerParams(vmem_limit_bytes=GRANT)
    state_spec = pl.BlockSpec((heads // groups, p_size, n), lambda g: (g, 0, 0))
    row_spec = pl.BlockSpec((1, of_group), lambda g: (0, g))
    weights = pltpu.with_memory_space_constraint(out_proj, pltpu.HBM)
    gain = norm_gain.reshape(1, width)

    def rows_of(x_in, z_gate, b_in, c_in, dt_raw, *_):
        return pl.pallas_call(
            pack_kernel,
            name="pack",
            out_shape=jax.ShapeDtypeStruct((2, width + groups * n + 2 * heads), BF16),
            compiler_params=params,
        )(x_in, z_gate, b_in, c_in, dt_raw)

    def beside(
        theirs, state, x_in, z_gate, b_in, c_in, dt_raw, dt_bias, a_log, d_skip, gain, weights, moves
    ):
        ends = theirs[:, width + groups * n :].astype(F32)
        their_dt = (ends[0, :heads] + ends[0, heads:]) + ends[1, :heads]
        step = jax.nn.softplus(jnp.stack([their_dt, dt_raw[0]]) + dt_bias)
        decay = jnp.exp(-jnp.exp(a_log) * step)
        each = jnp.stack([decay[0], step[0], d_skip, step[1]])
        per_head = jnp.repeat(each, p_size, axis=1)
        normed = pl.pallas_call(
            mix_kernel,
            name="mix",
            grid=(groups,),
            in_specs=[
                state_spec,
                pl.BlockSpec((2, of_group), lambda g: (0, g)),
                pl.BlockSpec((2, n), lambda g: (0, width // n + g)),
                pl.BlockSpec((4, of_group), lambda g: (0, g)),
                row_spec,
            ],
            out_specs=pl.BlockSpec((of_group // LANES, LANES), lambda g: (g, 0)),
            out_shape=jax.ShapeDtypeStruct((width // LANES, LANES), BF16),
            compiler_params=params,
        )(state.reshape(heads, p_size, n), theirs, theirs, per_head, gain)
        first_w, takes = pl.pallas_call(
            hold_kernel,
            name="hold",
            in_specs=[smem, hbm],
            out_specs=(vmem, vmem),
            out_shape=(
                pltpu.VMEM((weights.shape[0], FIRST * TILE), BF16),
                pltpu.VMEM((devices, devices), BF16),
            ),
            scratch_shapes=[pltpu.SemaphoreType.DMA],
            compiler_params=params,
        )(moves, pltpu.with_memory_space_constraint(weights, pltpu.HBM))
        return normed, first_w, takes, decay[1], per_head[3:4]

    operands = (x_in, z_gate, b_in, c_in, dt_raw, dt_bias, a_log, d_skip, gain, out_proj)
    if 2 * (devices - 1) <= MOST_PATTERNS and devices & (devices - 1) == 0:
        came, (normed, first_w, takes, decay, step) = pair_switch(
            index[0], devices, state, rows_of, beside, operands + (plan.T,)
        )
    else:
        came = spread_and_collect(state, source, target, devices)
        own = jnp.stack([target, target])
        normed, first_w, takes, decay, step = beside(rows_of(*operands), came, *operands, own)
    came = came.reshape(heads, p_size, n)

    block = width // devices
    lanes = min(block, LANES)
    mine = lax.all_to_all(
        normed.reshape(devices, block // lanes, lanes), AXIS, split_axis=0, concat_axis=0, tiled=True
    )

    new_state = pl.pallas_call(
        update_kernel,
        name="update",
        grid=(groups,),
        in_specs=[smem, smem, state_spec, row_spec, pl.BlockSpec((1, n), lambda g: (0, g)), row_spec],
        out_specs=state_spec,
        out_shape=jax.ShapeDtypeStruct((heads, p_size, n), BF16),
        compiler_params=params,
    )(live, decay, came, x_in, b_in, step)

    partial = pl.pallas_call(
        project_kernel,
        name="project",
        in_specs=[vmem, vmem, vmem, hbm],
        out_specs=vmem,
        out_shape=jax.ShapeDtypeStruct((devices, columns // LANES, LANES), BF16),
        scratch_shapes=[
            pltpu.VMEM((out_proj.shape[0], columns - FIRST * TILE), BF16),
            pltpu.SemaphoreType.DMA((columns // TILE - FIRST,)),
        ],
        compiler_params=params,
    )(in_vmem(takes), in_vmem(mine), in_vmem(first_w), weights)
    partial = lax.all_to_all(partial, AXIS, split_axis=0, concat_axis=0, tiled=True)
    mixed = pl.pallas_call(
        sum_kernel,
        name="total",
        in_specs=[vmem],
        out_shape=jax.ShapeDtypeStruct((1, columns), BF16),
        compiler_params=params,
    )(in_vmem(partial))
    return (mixed, new_state[None])


def solution(mesh):
    in_specs = (
        P(("groups", "dp"), None, None, None),
        P(("groups", "dp"), None),
        P(("groups", "dp"), None),
        P(("groups", "dp"), None),
        P(("groups", "dp"), None),
        P(("groups", "dp"), None),
        P(),
        P(),
        P(),
        P(),
        P("dp", None),
        P(("groups", "dp")),
        P("groups", None),
    )
    out_specs = (P(("groups", "dp"), None), P(("groups", "dp"), None, None, None))
    return jax.shard_map(local, mesh=mesh, in_specs=in_specs, out_specs=out_specs, check_vma=False)
```

```python
import functools

import jax
import jax.numpy as jnp
from jax import lax
from jax.experimental import pallas as pl
from jax.experimental.pallas import tpu as pltpu
from jax.sharding import PartitionSpec as P

AXIS = "dp"
LANES = 128
MOST_PATTERNS = 32
TILE = 1024
FIRST = 2
GRANT = 16 * 2**20
F32 = jnp.float32
BF16 = jnp.bfloat16


def pair_switch(index, devices, state, rows_of, beside, operands):
    def branch(distance, low_sends):
        pairs = [(i, i ^ distance) for i in range(devices) if (i < (i ^ distance)) == low_sends]
        back = [(t, s) for s, t in pairs]

        def move(state, operands):
            came = lax.ppermute(state, AXIS, pairs)
            theirs = lax.ppermute(rows_of(*operands), AXIS, back)
            return came, beside(theirs, state, *operands)

        return move

    branches = [branch(d, low) for d in range(1, devices) for low in (True, False)]
    return lax.switch(index, branches, state, operands)


def index_kernel(plan, index, live):
    me = lax.axis_index(AXIS)
    def move(k, found):
        partner, sends = found
        source, target = plan[0, k], plan[1, k]
        partner = jnp.where(source == me, target, jnp.where(target == me, source, partner))
        return partner, jnp.where(source == me, 1, sends)

    partner, sends = lax.fori_loop(0, plan.shape[1], move, (jnp.int32(0), jnp.int32(0)))
    low_sends = jnp.where(me < partner, sends, 1 - sends)
    index[0] = 2 * (jnp.bitwise_xor(me, partner) - 1) + 1 - low_sends
    live[0] = 1 - sends


def spread_and_collect(state, source, target, devices):
    ids = jnp.arange(devices, dtype=jnp.int32)
    matches = target[:, None] == ids[None, :]
    sender_of = jnp.sum(jnp.where(matches, source[:, None], 0), axis=0)
    has_sender = jnp.any(matches, axis=0)
    view = lax.all_to_all(state, AXIS, split_axis=1, concat_axis=0, tiled=True)
    routed = jnp.where(
        has_sender[:, None, None, None], jnp.take(view, sender_of, axis=0), jnp.zeros((), state.dtype)
    )
    return lax.all_to_all(routed, AXIS, split_axis=0, concat_axis=1, tiled=True)


def split(value):
    first = value.astype(BF16).astype(F32)
    second = (value - first).astype(BF16).astype(F32)
    return first, second, value - first - second


def pack_kernel(x, z, b, c, dt, out):
    first, second, third = split(dt[...])
    upper = [x[...].astype(F32), b[...].astype(F32), first, second]
    lower = [z[...].astype(F32), c[...].astype(F32), third, jnp.zeros_like(third)]
    at = 0
    for up, low in zip(upper, lower):
        width = up.shape[1]
        shape = (2, width)
        row = lax.broadcasted_iota(jnp.int32, shape, 0)
        both = jnp.where(row == 0, jnp.broadcast_to(up, shape), jnp.broadcast_to(low, shape))
        out[:, at : at + width] = both.astype(BF16)
        at += width


def mix_kernel(s, xz, bc, per_head, gain, out):
    heads, p_size, n = s.shape
    rows = bc[...].astype(F32)
    b, c = rows[0:1], rows[1:2]
    t = lax.dot_general(
        jnp.broadcast_to(c, (16, n)).astype(BF16),
        s[...].reshape(heads * p_size, n),
        (((1,), (1,)), ((), ())),
        preferred_element_type=F32,
    )[0:1]
    both = xz[...].astype(F32)
    x, z = both[0:1], both[1:2]
    y = (
        per_head[0:1] * t
        + (per_head[1:2] * x) * jnp.sum(b * c, axis=1, keepdims=True)
        + per_head[2:3] * x
    )
    gated = y * jax.nn.silu(z)
    factor = lax.rsqrt(jnp.mean(gated * gated, axis=1, keepdims=True) + 1e-05)
    normed = (gated * factor * gain[...]).astype(BF16).astype(F32)
    for q in range(normed.shape[1] // LANES):
        out[q : q + 1, :] = normed[:, q * LANES : (q + 1) * LANES]


def hold_kernel(moves, w, out, takes, sem):
    copy = pltpu.make_async_copy(w.at[:, pl.ds(0, out.shape[1])], out, sem)
    copy.start()
    to = lax.broadcasted_iota(jnp.int32, takes.shape, 0)
    of = lax.broadcasted_iota(jnp.int32, takes.shape, 1)

    def add(k, found):
        return jnp.where((of == moves[0, k]) & (to == moves[1, k]), 1.0, found)

    found = lax.fori_loop(0, moves.shape[1], add, jnp.zeros(takes.shape, F32))
    takes[...] = found.astype(BF16)
    copy.wait()


def update_kernel(live, decay, s, x, b, step, out):
    heads, p_size, n = out.shape
    g = pl.program_id(0)
    dx = step[...] * x[...].astype(F32)
    first, second, third = split(dx)
    row = lax.broadcasted_iota(jnp.int32, (16, dx.shape[1]), 0)
    terms = jnp.where(
        row == 0, first, jnp.where(row == 1, second, jnp.where(row == 2, third, 0.0))
    ).astype(BF16)
    outer = lax.dot_general(
        terms, jnp.broadcast_to(b[...], (16, n)), (((0,), (0,)), ((), ())), preferred_element_type=F32
    )
    for h in range(heads):
        fresh = decay[g * heads + h] * s[h].astype(F32) + outer[h * p_size : (h + 1) * p_size]
        out[h] = jnp.where(live[0] > 0, fresh, 0.0).astype(BF16)


def project_kernel(takes, rows, first_w, w, out, rest_w, sems):
    tiles = w.shape[1] // TILE
    have = first_w.shape[1] // TILE
    copies = [
        pltpu.make_async_copy(
            w.at[:, pl.ds((have + i) * TILE, TILE)], rest_w.at[:, pl.ds(i * TILE, TILE)], sems.at[i]
        )
        for i in range(tiles - have)
    ]
    for copy in copies:
        copy.start()
    lhs = jnp.concatenate([rows[:, r, :] for r in range(rows.shape[1])], axis=1).astype(BF16)
    lhs = jnp.dot(takes[...], lhs, preferred_element_type=F32).astype(BF16)
    for i in range(tiles):
        if i < have:
            weights = first_w[:, i * TILE : (i + 1) * TILE]
        else:
            copies[i - have].wait()
            weights = rest_w[:, (i - have) * TILE : (i - have + 1) * TILE]
        total = jnp.dot(lhs, weights, preferred_element_type=F32).astype(out.dtype)
        for j in range(TILE // LANES):
            out[:, i * (TILE // LANES) + j, :] = total[:, j * LANES : (j + 1) * LANES]


def sum_kernel(parts, out):
    total = jnp.sum(parts[...].astype(F32), axis=0).astype(BF16)
    for q in range(total.shape[0]):
        out[0:1, q * LANES : (q + 1) * LANES] = total[q : q + 1, :]


def local(
    state,
    x_in,
    z_gate,
    b_in,
    c_in,
    dt_raw,
    dt_bias,
    a_log,
    d_skip,
    norm_gain,
    out_proj,
    active,
    plan,
):
    devices = lax.axis_size(AXIS)
    heads, p_size, n = state.shape[1:]
    groups = b_in.shape[1] // n
    width = heads * p_size
    columns = out_proj.shape[1]
    source, target = plan[:, 0], plan[:, 1]
    smem = pl.BlockSpec(memory_space=pltpu.SMEM)
    index, live = pl.pallas_call(
        index_kernel,
        name="index",
        in_specs=[smem],
        out_specs=(smem, smem),
        out_shape=(pltpu.SMEM((1,), jnp.int32),) * 2,
    )(plan.T)

    of_group = width // groups
    vmem = pl.BlockSpec(memory_space=pltpu.VMEM)
    hbm = pl.BlockSpec(memory_space=pltpu.HBM)
    in_vmem = functools.partial(pltpu.with_memory_space_constraint, memory_space=pltpu.VMEM)
    params = pltpu.CompilerParams(vmem_limit_bytes=GRANT)
    state_spec = pl.BlockSpec((heads // groups, p_size, n), lambda g: (g, 0, 0))
    row_spec = pl.BlockSpec((1, of_group), lambda g: (0, g))
    in_hbm = functools.partial(pltpu.with_memory_space_constraint, memory_space=pltpu.HBM)
    weights = in_hbm(out_proj)
    gain = norm_gain.reshape(1, width)

    def rows_of(x_in, z_gate, b_in, c_in, dt_raw, *_):
        return pl.pallas_call(
            pack_kernel,
            name="pack",
            out_shape=jax.ShapeDtypeStruct((2, width + groups * n + 2 * heads), BF16),
            compiler_params=params,
        )(*[in_hbm(a) for a in (x_in, z_gate, b_in, c_in, dt_raw)])

    def beside(
        theirs, state, x_in, z_gate, b_in, c_in, dt_raw, dt_bias, a_log, d_skip, gain, weights, moves
    ):
        ends = theirs[:, width + groups * n :].astype(F32)
        their_dt = (ends[0, :heads] + ends[0, heads:]) + ends[1, :heads]
        step = jax.nn.softplus(jnp.stack([their_dt, dt_raw[0]]) + dt_bias)
        decay = jnp.exp(-jnp.exp(a_log) * step)
        each = jnp.stack([decay[0], step[0], d_skip, step[1]])
        per_head = jnp.repeat(each, p_size, axis=1)
        normed = pl.pallas_call(
            mix_kernel,
            name="mix",
            grid=(groups,),
            in_specs=[
                state_spec,
                pl.BlockSpec((2, of_group), lambda g: (0, g)),
                pl.BlockSpec((2, n), lambda g: (0, width // n + g)),
                pl.BlockSpec((4, of_group), lambda g: (0, g)),
                row_spec,
            ],
            out_specs=pl.BlockSpec((of_group // LANES, LANES), lambda g: (g, 0)),
            out_shape=jax.ShapeDtypeStruct((width // LANES, LANES), F32),
            compiler_params=params,
        )(state.reshape(heads, p_size, n), theirs, theirs, per_head, in_hbm(gain))
        first_w, takes = pl.pallas_call(
            hold_kernel,
            name="hold",
            in_specs=[smem, hbm],
            out_specs=(vmem, vmem),
            out_shape=(
                pltpu.VMEM((weights.shape[0], FIRST * TILE), BF16),
                pltpu.VMEM((devices, devices), BF16),
            ),
            scratch_shapes=[pltpu.SemaphoreType.DMA],
            compiler_params=params,
        )(moves, pltpu.with_memory_space_constraint(weights, pltpu.HBM))
        return normed, first_w, takes, decay[1], per_head[3:4]

    operands = (x_in, z_gate, b_in, c_in, dt_raw, dt_bias, a_log, d_skip, gain, out_proj)
    if 2 * (devices - 1) <= MOST_PATTERNS and devices & (devices - 1) == 0:
        came, (normed, first_w, takes, decay, step) = pair_switch(
            index[0], devices, state, rows_of, beside, operands + (plan.T,)
        )
    else:
        came = spread_and_collect(state, source, target, devices)
        own = jnp.stack([target, target])
        normed, first_w, takes, decay, step = beside(rows_of(*operands), came, *operands, own)
    came = came.reshape(heads, p_size, n)

    block = width // devices
    lanes = min(block, LANES)
    mine = lax.all_to_all(
        normed.reshape(devices, block // lanes, lanes), AXIS, split_axis=0, concat_axis=0, tiled=True
    )

    new_state = pl.pallas_call(
        update_kernel,
        name="update",
        grid=(groups,),
        in_specs=[smem, smem, state_spec, row_spec, pl.BlockSpec((1, n), lambda g: (0, g)), row_spec],
        out_specs=state_spec,
        out_shape=jax.ShapeDtypeStruct((heads, p_size, n), BF16),
        compiler_params=params,
    )(live, decay, came, x_in, b_in, step)

    partial = pl.pallas_call(
        project_kernel,
        name="project",
        in_specs=[vmem, vmem, vmem, hbm],
        out_specs=vmem,
        out_shape=jax.ShapeDtypeStruct((devices, columns // LANES, LANES), BF16),
        scratch_shapes=[
            pltpu.VMEM((out_proj.shape[0], columns - FIRST * TILE), BF16),
            pltpu.SemaphoreType.DMA((columns // TILE - FIRST,)),
        ],
        compiler_params=params,
    )(in_vmem(takes), in_vmem(mine), in_vmem(first_w), weights)
    partial = lax.all_to_all(partial, AXIS, split_axis=0, concat_axis=0, tiled=True)
    mixed = pl.pallas_call(
        sum_kernel,
        name="total",
        in_specs=[vmem],
        out_shape=jax.ShapeDtypeStruct((1, columns), BF16),
        compiler_params=params,
    )(in_vmem(partial))
    return (mixed, new_state[None])


def solution(mesh):
    in_specs = (
        P(("groups", "dp"), None, None, None),
        P(("groups", "dp"), None),
        P(("groups", "dp"), None),
        P(("groups", "dp"), None),
        P(("groups", "dp"), None),
        P(("groups", "dp"), None),
        P(),
        P(),
        P(),
        P(),
        P("dp", None),
        P(("groups", "dp")),
        P("groups", None),
    )
    out_specs = (P(("groups", "dp"), None), P(("groups", "dp"), None, None, None))
    return jax.shard_map(local, mesh=mesh, in_specs=in_specs, out_specs=out_specs, check_vma=False)
```

```python
import functools

import jax
import jax.numpy as jnp
from jax import lax
from jax.experimental import pallas as pl
from jax.experimental.pallas import tpu as pltpu
from jax.sharding import PartitionSpec as P

AXIS = "dp"
LANES = 128
MOST_PATTERNS = 32
TILE = 1024
FIRST = 3
GRANT = 16 * 2**20
F32 = jnp.float32
BF16 = jnp.bfloat16


def pair_switch(index, devices, state, rows_of, beside, operands):
    def branch(distance, low_sends):
        pairs = [(i, i ^ distance) for i in range(devices) if (i < (i ^ distance)) == low_sends]
        back = [(t, s) for s, t in pairs]

        def move(state, operands):
            came = lax.ppermute(state, AXIS, pairs)
            theirs = lax.ppermute(rows_of(*operands), AXIS, back)
            return came, beside(theirs, state, *operands)

        return move

    branches = [branch(d, low) for d in range(1, devices) for low in (True, False)]
    return lax.switch(index, branches, state, operands)


def index_kernel(me, plan, index, live):
    def move(k, found):
        partner, sends = found
        source, target = plan[0, k], plan[1, k]
        partner = jnp.where(source == me[0], target, jnp.where(target == me[0], source, partner))
        return partner, jnp.where(source == me[0], 1, sends)

    partner, sends = lax.fori_loop(0, plan.shape[1], move, (jnp.int32(0), jnp.int32(0)))
    low_sends = jnp.where(me[0] < partner, sends, 1 - sends)
    index[0] = 2 * (jnp.bitwise_xor(me[0], partner) - 1) + 1 - low_sends
    live[0] = 1 - sends


def spread_and_collect(state, source, target, devices):
    ids = jnp.arange(devices, dtype=jnp.int32)
    matches = target[:, None] == ids[None, :]
    sender_of = jnp.sum(jnp.where(matches, source[:, None], 0), axis=0)
    has_sender = jnp.any(matches, axis=0)
    view = lax.all_to_all(state, AXIS, split_axis=1, concat_axis=0, tiled=True)
    routed = jnp.where(
        has_sender[:, None, None, None], jnp.take(view, sender_of, axis=0), jnp.zeros((), state.dtype)
    )
    return lax.all_to_all(routed, AXIS, split_axis=0, concat_axis=1, tiled=True)


def split(value):
    first = value.astype(BF16).astype(F32)
    second = (value - first).astype(BF16).astype(F32)
    return first, second, value - first - second


def pack_kernel(x, z, b, c, dt, out):
    first, second, third = split(dt[...])
    upper = [x[...].astype(F32), b[...].astype(F32), first, second]
    lower = [z[...].astype(F32), c[...].astype(F32), third, jnp.zeros_like(third)]
    at = 0
    for up, low in zip(upper, lower):
        width = up.shape[1]
        shape = (2, width)
        row = lax.broadcasted_iota(jnp.int32, shape, 0)
        both = jnp.where(row == 0, jnp.broadcast_to(up, shape), jnp.broadcast_to(low, shape))
        out[:, at : at + width] = both.astype(BF16)
        at += width


def mix_kernel(s, xz, bc, per_head, gain, out):
    heads, p_size, n = s.shape
    rows = bc[...].astype(F32)
    b, c = rows[0:1], rows[1:2]
    t = lax.dot_general(
        jnp.broadcast_to(c, (16, n)).astype(BF16),
        s[...].reshape(heads * p_size, n),
        (((1,), (1,)), ((), ())),
        preferred_element_type=F32,
    )[0:1]
    both = xz[...].astype(F32)
    x, z = both[0:1], both[1:2]
    y = (
        per_head[0:1] * t
        + (per_head[1:2] * x) * jnp.sum(b * c, axis=1, keepdims=True)
        + per_head[2:3] * x
    )
    gated = y * jax.nn.silu(z)
    factor = lax.rsqrt(jnp.mean(gated * gated, axis=1, keepdims=True) + 1e-05)
    normed = (gated * factor * gain[...]).astype(BF16)
    for q in range(normed.shape[1] // LANES):
        out[q : q + 1, :] = normed[:, q * LANES : (q + 1) * LANES]


def hold_kernel(moves, w, out, takes, sem):
    copy = pltpu.make_async_copy(w.at[:, pl.ds(0, out.shape[1])], out, sem)
    copy.start()
    to = lax.broadcasted_iota(jnp.int32, takes.shape, 0)
    of = lax.broadcasted_iota(jnp.int32, takes.shape, 1)

    def add(k, found):
        return jnp.where((of == moves[0, k]) & (to == moves[1, k]), 1.0, found)

    found = lax.fori_loop(0, moves.shape[1], add, jnp.zeros(takes.shape, F32))
    takes[...] = found.astype(BF16)
    copy.wait()


def update_kernel(live, decay, s, x, b, step, out):
    heads, p_size, n = out.shape
    g = pl.program_id(0)
    dx = step[...] * x[...].astype(F32)
    first, second, third = split(dx)
    row = lax.broadcasted_iota(jnp.int32, (16, dx.shape[1]), 0)
    terms = jnp.where(
        row == 0, first, jnp.where(row == 1, second, jnp.where(row == 2, third, 0.0))
    ).astype(BF16)
    outer = lax.dot_general(
        terms, jnp.broadcast_to(b[...], (16, n)), (((0,), (0,)), ((), ())), preferred_element_type=F32
    )
    for h in range(heads):
        fresh = decay[g * heads + h] * s[h].astype(F32) + outer[h * p_size : (h + 1) * p_size]
        out[h] = jnp.where(live[0] > 0, fresh, 0.0).astype(BF16)


def project_kernel(takes, rows, first_w, w, out, rest_w, sems):
    tiles = w.shape[1] // TILE
    have = first_w.shape[1] // TILE
    copies = [
        pltpu.make_async_copy(
            w.at[:, pl.ds((have + i) * TILE, TILE)], rest_w.at[:, pl.ds(i * TILE, TILE)], sems.at[i]
        )
        for i in range(tiles - have)
    ]
    for copy in copies:
        copy.start()
    lhs = jnp.concatenate([rows[:, r, :] for r in range(rows.shape[1])], axis=1)
    lhs = jnp.dot(takes[...], lhs, preferred_element_type=F32).astype(BF16)
    for i in range(tiles):
        if i < have:
            weights = first_w[:, i * TILE : (i + 1) * TILE]
        else:
            copies[i - have].wait()
            weights = rest_w[:, (i - have) * TILE : (i - have + 1) * TILE]
        total = jnp.dot(lhs, weights, preferred_element_type=F32).astype(out.dtype)
        for j in range(TILE // LANES):
            out[:, i * (TILE // LANES) + j, :] = total[:, j * LANES : (j + 1) * LANES]


def sum_kernel(parts, out):
    total = jnp.sum(parts[...].astype(F32), axis=0).astype(BF16)
    for q in range(total.shape[0]):
        out[0:1, q * LANES : (q + 1) * LANES] = total[q : q + 1, :]


def local(
    state,
    x_in,
    z_gate,
    b_in,
    c_in,
    dt_raw,
    dt_bias,
    a_log,
    d_skip,
    norm_gain,
    out_proj,
    active,
    plan,
):
    devices = lax.axis_size(AXIS)
    me = lax.axis_index(AXIS)
    heads, p_size, n = state.shape[1:]
    groups = b_in.shape[1] // n
    width = heads * p_size
    columns = out_proj.shape[1]
    source, target = plan[:, 0], plan[:, 1]
    smem = pl.BlockSpec(memory_space=pltpu.SMEM)
    index, live = pl.pallas_call(
        index_kernel,
        name="index",
        in_specs=[smem, smem],
        out_specs=(smem, smem),
        out_shape=(pltpu.SMEM((1,), jnp.int32),) * 2,
    )(me.astype(jnp.int32).reshape(1), plan.T)

    of_group = width // groups
    vmem = pl.BlockSpec(memory_space=pltpu.VMEM)
    hbm = pl.BlockSpec(memory_space=pltpu.HBM)
    in_vmem = functools.partial(pltpu.with_memory_space_constraint, memory_space=pltpu.VMEM)
    params = pltpu.CompilerParams(vmem_limit_bytes=GRANT)
    state_spec = pl.BlockSpec((heads // groups, p_size, n), lambda g: (g, 0, 0))
    row_spec = pl.BlockSpec((1, of_group), lambda g: (0, g))
    weights = pltpu.with_memory_space_constraint(out_proj, pltpu.HBM)
    gain = norm_gain.reshape(1, width)

    def rows_of(x_in, z_gate, b_in, c_in, dt_raw, *_):
        return pl.pallas_call(
            pack_kernel,
            name="pack",
            out_shape=jax.ShapeDtypeStruct((2, width + groups * n + 2 * heads), BF16),
            compiler_params=params,
        )(x_in, z_gate, b_in, c_in, dt_raw)

    def beside(
        theirs, state, x_in, z_gate, b_in, c_in, dt_raw, dt_bias, a_log, d_skip, gain, weights, moves
    ):
        ends = theirs[:, width + groups * n :].astype(F32)
        their_dt = (ends[0, :heads] + ends[0, heads:]) + ends[1, :heads]
        step = jax.nn.softplus(jnp.stack([their_dt, dt_raw[0]]) + dt_bias)
        decay = jnp.exp(-jnp.exp(a_log) * step)
        each = jnp.stack([decay[0], step[0], d_skip, step[1]])
        per_head = jnp.repeat(each, p_size, axis=1)
        normed = pl.pallas_call(
            mix_kernel,
            name="mix",
            grid=(groups,),
            in_specs=[
                state_spec,
                pl.BlockSpec((2, of_group), lambda g: (0, g)),
                pl.BlockSpec((2, n), lambda g: (0, width // n + g)),
                pl.BlockSpec((4, of_group), lambda g: (0, g)),
                row_spec,
            ],
            out_specs=pl.BlockSpec((of_group // LANES, LANES), lambda g: (g, 0)),
            out_shape=jax.ShapeDtypeStruct((width // LANES, LANES), BF16),
            compiler_params=params,
        )(state.reshape(heads, p_size, n), theirs, theirs, per_head, gain)
        first_w, takes = pl.pallas_call(
            hold_kernel,
            name="hold",
            in_specs=[smem, hbm],
            out_specs=(vmem, vmem),
            out_shape=(
                pltpu.VMEM((weights.shape[0], FIRST * TILE), BF16),
                pltpu.VMEM((devices, devices), BF16),
            ),
            scratch_shapes=[pltpu.SemaphoreType.DMA],
            compiler_params=params,
        )(moves, pltpu.with_memory_space_constraint(weights, pltpu.HBM))
        return normed, first_w, takes, decay[1], per_head[3:4]

    operands = (x_in, z_gate, b_in, c_in, dt_raw, dt_bias, a_log, d_skip, gain, out_proj)
    if 2 * (devices - 1) <= MOST_PATTERNS and devices & (devices - 1) == 0:
        came, (normed, first_w, takes, decay, step) = pair_switch(
            index[0], devices, state, rows_of, beside, operands + (plan.T,)
        )
    else:
        came = spread_and_collect(state, source, target, devices)
        own = jnp.stack([target, target])
        normed, first_w, takes, decay, step = beside(rows_of(*operands), came, *operands, own)
    came = came.reshape(heads, p_size, n)

    block = width // devices
    lanes = min(block, LANES)
    mine = lax.all_to_all(
        normed.reshape(devices, block // lanes, lanes), AXIS, split_axis=0, concat_axis=0, tiled=True
    )

    new_state = pl.pallas_call(
        update_kernel,
        name="update",
        grid=(groups,),
        in_specs=[smem, smem, state_spec, row_spec, pl.BlockSpec((1, n), lambda g: (0, g)), row_spec],
        out_specs=state_spec,
        out_shape=jax.ShapeDtypeStruct((heads, p_size, n), BF16),
        compiler_params=params,
    )(live, decay, came, x_in, b_in, step)

    partial = pl.pallas_call(
        project_kernel,
        name="project",
        in_specs=[vmem, vmem, vmem, hbm],
        out_specs=vmem,
        out_shape=jax.ShapeDtypeStruct((devices, columns // LANES, LANES), BF16),
        scratch_shapes=[
            pltpu.VMEM((out_proj.shape[0], columns - FIRST * TILE), BF16),
            pltpu.SemaphoreType.DMA((columns // TILE - FIRST,)),
        ],
        compiler_params=params,
    )(in_vmem(takes), in_vmem(mine), in_vmem(first_w), weights)
    partial = lax.all_to_all(partial, AXIS, split_axis=0, concat_axis=0, tiled=True)
    mixed = pl.pallas_call(
        sum_kernel,
        name="total",
        in_specs=[vmem],
        out_shape=jax.ShapeDtypeStruct((1, columns), BF16),
        compiler_params=params,
    )(in_vmem(partial))
    return (mixed, new_state[None])


def solution(mesh):
    in_specs = (
        P(("groups", "dp"), None, None, None),
        P(("groups", "dp"), None),
        P(("groups", "dp"), None),
        P(("groups", "dp"), None),
        P(("groups", "dp"), None),
        P(("groups", "dp"), None),
        P(),
        P(),
        P(),
        P(),
        P("dp", None),
        P(("groups", "dp")),
        P("groups", None),
    )
    out_specs = (P(("groups", "dp"), None), P(("groups", "dp"), None, None, None))
    return jax.shard_map(local, mesh=mesh, in_specs=in_specs, out_specs=out_specs, check_vma=False)
```
